32 devices in a mesh: sector: 8 (over y, x, core), term: 4 (over z).
Axes of the slice: x: 2, y: 2, z: 4, core: 2. Of those that a mesh axis runs over, the one named last changes fastest.
Arguments:
- blocks: bfloat16 [5120, 640], P('sector'), may hold values from -6 to 6
- left_env: bfloat16 [8, 4, 640, 1920], P('sector', 'term'), may hold values from -0.125 to 0.125
- right_env: bfloat16 [8, 4, 640, 640], P('sector', 'term'), may hold values from -0.125 to 0.125
- coupling: int32 [8, 3], P('sector'), may hold values 0 or 1
- widths: int32 [8], P('sector'), may hold values from 320 to 640
Outputs:
- filtered: bfloat16 [5120, 640], P('sector')
The draws below stay inside these ranges and needn't reach their ends.
All inputs are finite; a program needn't handle non-finite values. No bound on the sum of `coupling` on one device may be relied on, other than what follows from the above.
Results may differ from the reference program's by a relative error of at most 0.005.
Values may be sent and summed in bfloat16 or wider, within the bound.
A program may use at most 64 MiB of HBM per device.

```python
import jax
import jax.numpy as jnp
from jax import lax

P_SIZE = 640
COUPLED = 3
SECTORS = 8
TERMS = 4


def with_ends(entries, key, least, high):
    shape = entries.shape
    index_at = [jax.random.randint(jax.random.fold_in(key, axis), (), 0, shape[axis]) for axis in range(len(shape))]
    entries = entries.at[tuple(index_at)].set(least)
    longest = shape.index(max(shape))
    index_at[longest] = (index_at[longest] + 1) % shape[longest]
    return entries.at[tuple(index_at)].set(high)


def block_scale(own_key, dims, cuts, low, largest):
    def one(dim, shards_of):
        draws = jax.random.uniform(jax.random.fold_in(jax.random.fold_in(own_key, 6), dim), (shards_of,), jnp.float32, low / len(cuts), largest / len(cuts))
        return jnp.repeat(jnp.exp(draws), dims[dim] // shards_of).reshape((-1,) + (1,) * (len(dims) - dim - 1))

    factor_of = one(*cuts[0])
    for cut in cuts[1:]:
        factor_of = factor_of * one(*cut)
    return factor_of


def scatter_about(rng, extent, scale, most, cuts=(), kind=jnp.bfloat16):
    loudness = block_scale(rng, extent, cuts, -0.22, 0.18) if cuts else 1.0
    drawn = jax.random.normal(rng, extent, jnp.float32) * scale * loudness
    return jnp.minimum(jnp.maximum(drawn, -most), most).astype(kind)


def setup_inputs(seed: int = 0) -> dict:
    key_list = jax.random.split(jax.random.key(seed), 6)
    blocks = scatter_about(key_list[0], (SECTORS * P_SIZE, P_SIZE), 1.0, 6.0, ((0, 8),))
    left_env = scatter_about(key_list[1], (SECTORS, TERMS, P_SIZE, COUPLED * P_SIZE), (COUPLED * P_SIZE) ** -0.5, 0.125, ((0, 8), (1, 4)))
    right_env = scatter_about(key_list[2], (SECTORS, TERMS, P_SIZE, P_SIZE), (P_SIZE * TERMS) ** -0.5, 0.125, ((0, 8), (1, 4)))
    coupling = with_ends((jax.random.randint(key_list[3], (SECTORS, COUPLED), 0, 4) < 3).astype(jnp.int32), jax.random.fold_in(key_list[3], 1), 0, 1)
    widths = with_ends(jax.random.randint(key_list[4], (SECTORS,), P_SIZE // 2, P_SIZE + 1), jax.random.fold_in(key_list[4], 1), P_SIZE // 2, P_SIZE).astype(jnp.int32)
    return dict(blocks=blocks, left_env=left_env, right_env=right_env, coupling=coupling, widths=widths)


def keep_live(values, live_width, row_offset):
    row_index = row_offset + lax.broadcasted_iota(jnp.int32, values.shape, 0)
    col_index = lax.broadcasted_iota(jnp.int32, values.shape, 1)
    return jnp.where((row_index < live_width) & (col_index < live_width), values, jnp.zeros_like(values))


def apply_operator(source, left_env, right_env, coupling, widths):
    zero_block = jnp.zeros((1, P_SIZE, P_SIZE), source.dtype)
    padded = jnp.concatenate([zero_block, source, zero_block], axis=0)
    nearby = jnp.stack([padded[:-2], padded[1:-1], padded[2:]], axis=1)

    def per_sector(pieces):
        left_part, right_part, nearby_part, coupled, live_width = pieces
        scaled = nearby_part * coupled.astype(source.dtype)[:, None, None]
        stacked = scaled.reshape(COUPLED * P_SIZE, P_SIZE).astype(jnp.float32)
        partial_value = jnp.einsum("tik,kj->tij", left_part.astype(jnp.float32), stacked).astype(jnp.bfloat16)
        summed = jnp.einsum("tij,tjl->il", partial_value.astype(jnp.float32), right_part.astype(jnp.float32))
        return keep_live(summed, live_width, 0)

    return lax.map(per_sector, (left_env, right_env, nearby, coupling, widths))


def reference(blocks, left_env, right_env, coupling, widths):
    source = blocks.reshape(SECTORS, P_SIZE, P_SIZE)
    first_pass = apply_operator(source, left_env, right_env, coupling, widths).astype(jnp.bfloat16)
    second = apply_operator(first_pass, left_env, right_env, coupling, widths)
    filtered = (2.0 * second - source.astype(jnp.float32)).astype(jnp.bfloat16)
    return filtered.reshape(SECTORS * P_SIZE, P_SIZE)
```

```python
import functools

import jax
import jax.numpy as jnp
from jax import lax
from jax.experimental import pallas as pl
from jax.experimental.pallas import tpu as pltpu
from jax.sharding import PartitionSpec as P

MESH = pl.DeviceIdType.MESH
PIECE = 32


def kernel(n_s, n_t, pieces, blocks_ref, left_ref, right_ref, coup_ref, width_ref, out_ref,
           lbuf, rbuf, st1, st2, sbuf, recv, send, obuf,
           lsem, osem, h1s, h1r, rss, rsr, ags, agr, h2s, h2r):
    s = lax.axis_index("sector")
    z = lax.axis_index("term")
    side = blocks_ref.shape[0]
    half = side // 2
    pr = half // pieces
    has_lo, has_hi = s > 0, s < n_s - 1
    has_dn, has_up = z > 0, z < n_t - 1

    def to_sector(d):
        return (s + d, z)

    own1 = st1.at[pl.ds(side, side), :]
    cp_own = pltpu.make_async_copy(blocks_ref, own1, lsem.at[0])
    cp_l = pltpu.make_async_copy(left_ref.at[0, 0], lbuf, lsem.at[1])
    cp_r = pltpu.make_async_copy(right_ref.at[0, 0], rbuf, lsem.at[2])
    cp_own.start()
    cp_l.start()
    cp_r.start()

    barrier = pltpu.get_barrier_semaphore()
    for cond, dev in ((has_lo, (s - 1, z)), (has_hi, (s + 1, z)), (has_dn, (s, z - 1)), (has_up, (s, z + 1))):
        @pl.when(cond)
        def _():
            pl.semaphore_signal(barrier, inc=1, device_id=dev, device_id_type=MESH)
    count = (has_lo.astype(jnp.int32) + has_hi.astype(jnp.int32)
             + has_dn.astype(jnp.int32) + has_up.astype(jnp.int32))
    pl.semaphore_wait(barrier, count)

    def halo1(d):
        group = 2 if d < 0 else 0
        slot = 0 if d < 0 else 1
        return pltpu.make_async_remote_copy(
            src_ref=blocks_ref, dst_ref=st1.at[pl.ds(group * side, side), :],
            send_sem=h1s.at[slot], recv_sem=h1r.at[slot],
            device_id=to_sector(d), device_id_type=MESH)

    @pl.when(has_lo)
    def _():
        halo1(-1).start()

    @pl.when(has_hi)
    def _():
        halo1(1).start()

    zeros = jnp.zeros((side, side), st1.dtype)

    @pl.when(jnp.logical_not(has_lo))
    def _():
        st1[pl.ds(0, side), :] = zeros
        st2[pl.ds(0, side), :] = zeros

    @pl.when(jnp.logical_not(has_hi))
    def _():
        st1[pl.ds(2 * side, side), :] = zeros
        st2[pl.ds(2 * side, side), :] = zeros

    width = width_ref[0]
    cp_l.wait()
    for k in range(3):
        c = coup_ref[0, k].astype(jnp.float32)
        cols = pl.ds(k * side, side)
        lbuf[:, cols] = (lbuf[:, cols].astype(jnp.float32) * c).astype(lbuf.dtype)
    cp_own.wait()
    cp_r.wait()

    x = jnp.where(z * 2 < n_t, 1, 0)
    flows = (x, 1 - x)

    def has_prev(f):
        return jnp.where(f == 1, z, n_t - 1 - z) > 0

    def has_next(f):
        return jnp.where(f == 1, n_t - 1 - z, z) > 0

    def rows_of(f, i):
        return pl.ds(pl.multiple_of(f * half + i * pr, pr), pr)

    def contract(st, f):
        base = pl.ds(pl.multiple_of(f * half, half), half)
        t = jnp.dot(lbuf[base, :], st[...], preferred_element_type=jnp.float32).astype(jnp.bfloat16)
        sbuf[base, :] = jnp.dot(t, rbuf[...], preferred_element_type=jnp.float32)

    def rs_copy(a, f, i):
        r = rows_of(f, i)
        return pltpu.make_async_remote_copy(
            src_ref=send.at[a, r, :], dst_ref=recv.at[a, r, :],
            send_sem=rss.at[a, f, i], recv_sem=rsr.at[a, f, i],
            device_id=(s, z + 2 * f - 1), device_id_type=MESH)

    def result(a, f, i):
        if a == 0:
            return st2.at[pl.ds(pl.multiple_of(side + f * half + i * pr, pr), pr), :]
        return obuf.at[rows_of(f, i), :]

    def ag_copy(a, f, i):
        return pltpu.make_async_remote_copy(
            src_ref=result(a, f, i), dst_ref=result(a, f, i),
            send_sem=ags.at[a, f, i], recv_sem=agr.at[a, f, i],
            device_id=(s, z - 2 * f + 1), device_id_type=MESH)

    def halo2(d, f, i):
        group = 2 if d < 0 else 0
        slot = 0 if d < 0 else 1
        dst = pl.ds(pl.multiple_of(group * side + f * half + i * pr, pr), pr)
        return pltpu.make_async_remote_copy(
            src_ref=result(0, f, i), dst_ref=st2.at[dst, :],
            send_sem=h2s.at[slot, f, i], recv_sem=h2r.at[slot, f, i],
            device_id=to_sector(d), device_id_type=MESH)

    def out_copy(f, i):
        return pltpu.make_async_copy(obuf.at[rows_of(f, i), :], out_ref.at[rows_of(f, i), :], osem.at[f, i])

    def publish(a, f, i):
        if a == 0:
            @pl.when(has_lo)
            def _():
                halo2(-1, f, i).start()

            @pl.when(has_hi)
            def _():
                halo2(1, f, i).start()
        else:
            out_copy(f, i).start()

    def reduce_step(a, f, i):
        r = rows_of(f, i)

        @pl.when(has_prev(f))
        def _():
            rs_copy(a, f, i).wait_recv()
            sbuf[r, :] = sbuf[r, :] + recv[a, r, :].astype(jnp.float32)

        @pl.when(has_next(f))
        def _():
            send[a, r, :] = sbuf[r, :].astype(send.dtype)
            rs_copy(a, f, i).start()

        @pl.when(jnp.logical_not(has_next(f)))
        def _():
            value = sbuf[r, :]
            row = f * half + i * pr + lax.broadcasted_iota(jnp.int32, value.shape, 0)
            col = lax.broadcasted_iota(jnp.int32, value.shape, 1)
            value = jnp.where((row < width) & (col < width), value, jnp.zeros_like(value))
            if a == 1:
                start = st1[pl.ds(pl.multiple_of(side + f * half + i * pr, pr), pr), :]
                value = 2.0 * value - start.astype(jnp.float32)
            result(a, f, i)[...] = value.astype(st2.dtype)

            @pl.when(has_prev(f))
            def _():
                ag_copy(a, f, i).start()
            publish(a, f, i)

    def gather_step(a, f, i):
        @pl.when(has_next(f))
        def _():
            ag_copy(a, f, i).wait_recv()

            @pl.when(has_prev(f))
            def _():
                ag_copy(a, f, i).start()
            publish(a, f, i)

    def loop(body):
        def step(i, c):
            body(i)
            return c
        lax.fori_loop(0, pieces, step, 0)

    def apply(a, st):
        fx, fy = flows
        contract(st, fx)

        @pl.when(jnp.logical_not(has_prev(fx)))
        def _():
            loop(lambda i: reduce_step(a, fx, i))

        contract(st, fy)

        def both(i):
            @pl.when(has_prev(fx))
            def _():
                reduce_step(a, fx, i)
            reduce_step(a, fy, i)
        loop(both)

        def gather(i):
            gather_step(a, fy, i)
            gather_step(a, fx, i)
        loop(gather)

    @pl.when(has_lo)
    def _():
        halo1(1).wait_recv()

    @pl.when(has_hi)
    def _():
        halo1(-1).wait_recv()
    apply(0, st1)

    def arrived(i):
        for f in flows:
            @pl.when(has_lo)
            def _():
                halo2(1, f, i).wait_recv()

            @pl.when(has_hi)
            def _():
                halo2(-1, f, i).wait_recv()
    loop(arrived)
    apply(1, st2)

    def drain(i):
        for f in (0, 1):
            for a in (0, 1):
                @pl.when(has_next(f))
                def _():
                    rs_copy(a, f, i).wait_send()

                @pl.when(has_prev(f))
                def _():
                    ag_copy(a, f, i).wait_send()

            @pl.when(has_lo)
            def _():
                halo2(-1, f, i).wait_send()

            @pl.when(has_hi)
            def _():
                halo2(1, f, i).wait_send()
            out_copy(f, i).wait()
    loop(drain)

    @pl.when(has_lo)
    def _():
        halo1(-1).wait_send()

    @pl.when(has_hi)
    def _():
        halo1(1).wait_send()


def shards(n_s, n_t, blocks, left_env, right_env, coupling, widths):
    side = blocks.shape[1]
    pieces = side // 2 // PIECE
    dma = pltpu.SemaphoreType.DMA
    any_space = pl.BlockSpec(memory_space=pl.ANY)
    smem = pl.BlockSpec(memory_space=pltpu.SMEM)
    return pl.pallas_call(
        functools.partial(kernel, n_s, n_t, pieces),
        out_shape=jax.ShapeDtypeStruct(blocks.shape, blocks.dtype),
        in_specs=[any_space, any_space, any_space, smem, smem],
        out_specs=any_space,
        scratch_shapes=[
            pltpu.VMEM((side, 3 * side), jnp.bfloat16),
            pltpu.VMEM((side, side), jnp.bfloat16),
            pltpu.VMEM((3 * side, side), jnp.bfloat16),
            pltpu.VMEM((3 * side, side), jnp.bfloat16),
            pltpu.VMEM((side, side), jnp.float32),
            pltpu.VMEM((2, side, side), jnp.bfloat16),
            pltpu.VMEM((2, side, side), jnp.bfloat16),
            pltpu.VMEM((side, side), jnp.bfloat16),
            dma((3,)), dma((2, pieces)), dma((2,)), dma((2,)),
            dma((2, 2, pieces)), dma((2, 2, pieces)),
            dma((2, 2, pieces)), dma((2, 2, pieces)),
            dma((2, 2, pieces)), dma((2, 2, pieces)),
        ],
        compiler_params=pltpu.CompilerParams(collective_id=0, has_side_effects=True),
    )(blocks, left_env, right_env, coupling, widths)


def solution(mesh):
    placed = (
        P("sector", None),
        P("sector", "term", None, None),
        P("sector", "term", None, None),
        P("sector", None),
        P("sector"),
    )
    body = functools.partial(shards, mesh.shape["sector"], mesh.shape["term"])
    return jax.shard_map(body, mesh=mesh, in_specs=placed, out_specs=P("sector", None), check_vma=False)
```

```python
import functools

import jax
import jax.numpy as jnp
from jax import lax
from jax.experimental import pallas as pl
from jax.experimental.pallas import tpu as pltpu
from jax.sharding import PartitionSpec as P

MESH = pl.DeviceIdType.MESH
PIECE = 32
LAG = 4


def kernel(n_s, n_t, pieces, blocks_ref, left_ref, right_ref, coup_ref, width_ref, out_ref,
           lbuf, rbuf, st1, st2, sbuf, recv, send, obuf,
           lsem, osem, h1s, h1r, rss, rsr, ags, agr, h2s, h2r):
    s = lax.axis_index("sector")
    z = lax.axis_index("term")
    side = blocks_ref.shape[0]
    half = side // 2
    pr = half // pieces
    has_lo, has_hi = s > 0, s < n_s - 1
    has_dn, has_up = z > 0, z < n_t - 1

    def to_sector(d):
        return (s + d, z)

    own1 = st1.at[pl.ds(side, side), :]
    cp_own = pltpu.make_async_copy(blocks_ref, own1, lsem.at[0])
    cp_l = pltpu.make_async_copy(left_ref.at[0, 0], lbuf, lsem.at[1])
    cp_r = pltpu.make_async_copy(right_ref.at[0, 0], rbuf, lsem.at[2])
    cp_own.start()
    cp_l.start()
    cp_r.start()

    barrier = pltpu.get_barrier_semaphore()
    for cond, dev in ((has_lo, (s - 1, z)), (has_hi, (s + 1, z)), (has_dn, (s, z - 1)), (has_up, (s, z + 1))):
        @pl.when(cond)
        def _():
            pl.semaphore_signal(barrier, inc=1, device_id=dev, device_id_type=MESH)
    count = (has_lo.astype(jnp.int32) + has_hi.astype(jnp.int32)
             + has_dn.astype(jnp.int32) + has_up.astype(jnp.int32))
    pl.semaphore_wait(barrier, count)

    def halo1(d):
        group = 2 if d < 0 else 0
        slot = 0 if d < 0 else 1
        return pltpu.make_async_remote_copy(
            src_ref=blocks_ref, dst_ref=st1.at[pl.ds(group * side, side), :],
            send_sem=h1s.at[slot], recv_sem=h1r.at[slot],
            device_id=to_sector(d), device_id_type=MESH)

    @pl.when(has_lo)
    def _():
        halo1(-1).start()

    @pl.when(has_hi)
    def _():
        halo1(1).start()

    zeros = jnp.zeros((side, side), st1.dtype)

    @pl.when(jnp.logical_not(has_lo))
    def _():
        st1[pl.ds(0, side), :] = zeros
        st2[pl.ds(0, side), :] = zeros

    @pl.when(jnp.logical_not(has_hi))
    def _():
        st1[pl.ds(2 * side, side), :] = zeros
        st2[pl.ds(2 * side, side), :] = zeros

    width = width_ref[0]
    cp_l.wait()
    for k in range(3):
        c = coup_ref[0, k].astype(jnp.float32)
        cols = pl.ds(k * side, side)
        lbuf[:, cols] = (lbuf[:, cols].astype(jnp.float32) * c).astype(lbuf.dtype)
    cp_own.wait()
    cp_r.wait()

    x = jnp.where(z * 2 < n_t, 1, 0)
    flows = (x, 1 - x)

    def far(f):
        return jnp.where(f == 1, z, n_t - 1 - z)

    def has_prev(f):
        return far(f) > 0

    def has_next(f):
        return jnp.where(f == 1, n_t - 1 - z, z) > 0

    def rows_of(f, i):
        return pl.ds(pl.multiple_of(f * half + i * pr, pr), pr)

    def contract(st, f):
        base = pl.ds(pl.multiple_of(f * half, half), half)
        t = jnp.dot(lbuf[base, :], st[...], preferred_element_type=jnp.float32).astype(jnp.bfloat16)
        sbuf[base, :] = jnp.dot(t, rbuf[...], preferred_element_type=jnp.float32)

    def rs_copy(a, f, i):
        r = rows_of(f, i)
        return pltpu.make_async_remote_copy(
            src_ref=send.at[a, r, :], dst_ref=recv.at[a, r, :],
            send_sem=rss.at[a, f, i], recv_sem=rsr.at[a, f, i],
            device_id=(s, z + 2 * f - 1), device_id_type=MESH)

    def result(a, f, i):
        if a == 0:
            return st2.at[pl.ds(pl.multiple_of(side + f * half + i * pr, pr), pr), :]
        return obuf.at[rows_of(f, i), :]

    def ag_copy(a, f, i):
        return pltpu.make_async_remote_copy(
            src_ref=result(a, f, i), dst_ref=result(a, f, i),
            send_sem=ags.at[a, f, i], recv_sem=agr.at[a, f, i],
            device_id=(s, z - 2 * f + 1), device_id_type=MESH)

    def halo2(d, f, i):
        group = 2 if d < 0 else 0
        slot = 0 if d < 0 else 1
        dst = pl.ds(pl.multiple_of(group * side + f * half + i * pr, pr), pr)
        return pltpu.make_async_remote_copy(
            src_ref=result(0, f, i), dst_ref=st2.at[dst, :],
            send_sem=h2s.at[slot, f, i], recv_sem=h2r.at[slot, f, i],
            device_id=to_sector(d), device_id_type=MESH)

    def out_copy(f, i):
        return pltpu.make_async_copy(obuf.at[rows_of(f, i), :], out_ref.at[rows_of(f, i), :], osem.at[f, i])

    def publish(a, f, i):
        if a == 0:
            @pl.when(has_lo)
            def _():
                halo2(-1, f, i).start()

            @pl.when(has_hi)
            def _():
                halo2(1, f, i).start()
        else:
            out_copy(f, i).start()

    def reduce_step(a, f, i):
        r = rows_of(f, i)

        @pl.when(has_prev(f))
        def _():
            rs_copy(a, f, i).wait_recv()
            sbuf[r, :] = sbuf[r, :] + recv[a, r, :].astype(jnp.float32)

        @pl.when(has_next(f))
        def _():
            send[a, r, :] = sbuf[r, :].astype(send.dtype)
            rs_copy(a, f, i).start()

        @pl.when(jnp.logical_not(has_next(f)))
        def _():
            value = sbuf[r, :]
            row = f * half + i * pr + lax.broadcasted_iota(jnp.int32, value.shape, 0)
            col = lax.broadcasted_iota(jnp.int32, value.shape, 1)
            value = jnp.where((row < width) & (col < width), value, jnp.zeros_like(value))
            if a == 1:
                start = st1[pl.ds(pl.multiple_of(side + f * half + i * pr, pr), pr), :]
                value = 2.0 * value - start.astype(jnp.float32)
            result(a, f, i)[...] = value.astype(st2.dtype)

            @pl.when(has_prev(f))
            def _():
                ag_copy(a, f, i).start()
            publish(a, f, i)

    def gather_step(a, f, i):
        @pl.when(has_next(f))
        def _():
            ag_copy(a, f, i).wait_recv()

            @pl.when(has_prev(f))
            def _():
                ag_copy(a, f, i).start()
            publish(a, f, i)

    def loop(body):
        def step(i, c):
            body(i)
            return c
        lax.fori_loop(0, pieces, step, 0)

    def apply(a, st):
        fx, fy = flows
        contract(st, fx)

        @pl.when(jnp.logical_not(has_prev(fx)))
        def _():
            loop(lambda i: reduce_step(a, fx, i))

        contract(st, fy)

        def slot(t, c):
            for f in (fy, fx):
                i = t - (2 * (n_t - 1) - far(f)) * LAG

                @pl.when((i >= 0) & (i < pieces))
                def _():
                    gather_step(a, f, i)
            for f in (fy, fx):
                i = t - far(f) * LAG
                ready = (i >= 0) & (i < pieces)

                @pl.when(ready & has_prev(f) if f is fx else ready)
                def _():
                    reduce_step(a, f, i)
            return c
        lax.fori_loop(0, 2 * (n_t - 1) * LAG + pieces, slot, 0)

    @pl.when(has_lo)
    def _():
        halo1(1).wait_recv()

    @pl.when(has_hi)
    def _():
        halo1(-1).wait_recv()
    apply(0, st1)

    def arrived(i):
        for f in flows:
            @pl.when(has_lo)
            def _():
                halo2(1, f, i).wait_recv()

            @pl.when(has_hi)
            def _():
                halo2(-1, f, i).wait_recv()
    loop(arrived)
    apply(1, st2)

    def drain(i):
        for f in (0, 1):
            for a in (0, 1):
                @pl.when(has_next(f))
                def _():
                    rs_copy(a, f, i).wait_send()

                @pl.when(has_prev(f))
                def _():
                    ag_copy(a, f, i).wait_send()

            @pl.when(has_lo)
            def _():
                halo2(-1, f, i).wait_send()

            @pl.when(has_hi)
            def _():
                halo2(1, f, i).wait_send()
            out_copy(f, i).wait()
    loop(drain)

    @pl.when(has_lo)
    def _():
        halo1(-1).wait_send()

    @pl.when(has_hi)
    def _():
        halo1(1).wait_send()


def shards(n_s, n_t, blocks, left_env, right_env, coupling, widths):
    side = blocks.shape[1]
    pieces = side // 2 // PIECE
    dma = pltpu.SemaphoreType.DMA
    any_space = pl.BlockSpec(memory_space=pl.ANY)
    smem = pl.BlockSpec(memory_space=pltpu.SMEM)
    return pl.pallas_call(
        functools.partial(kernel, n_s, n_t, pieces),
        out_shape=jax.ShapeDtypeStruct(blocks.shape, blocks.dtype),
        in_specs=[any_space, any_space, any_space, smem, smem],
        out_specs=any_space,
        scratch_shapes=[
            pltpu.VMEM((side, 3 * side), jnp.bfloat16),
            pltpu.VMEM((side, side), jnp.bfloat16),
            pltpu.VMEM((3 * side, side), jnp.bfloat16),
            pltpu.VMEM((3 * side, side), jnp.bfloat16),
            pltpu.VMEM((side, side), jnp.float32),
            pltpu.VMEM((2, side, side), jnp.bfloat16),
            pltpu.VMEM((2, side, side), jnp.bfloat16),
            pltpu.VMEM((side, side), jnp.bfloat16),
            dma((3,)), dma((2, pieces)), dma((2,)), dma((2,)),
            dma((2, 2, pieces)), dma((2, 2, pieces)),
            dma((2, 2, pieces)), dma((2, 2, pieces)),
            dma((2, 2, pieces)), dma((2, 2, pieces)),
        ],
        compiler_params=pltpu.CompilerParams(collective_id=0, has_side_effects=True),
    )(blocks, left_env, right_env, coupling, widths)


def solution(mesh):
    placed = (
        P("sector", None),
        P("sector", "term", None, None),
        P("sector", "term", None, None),
        P("sector", None),
        P("sector"),
    )
    body = functools.partial(shards, mesh.shape["sector"], mesh.shape["term"])
    return jax.shard_map(body, mesh=mesh, in_specs=placed, out_specs=P("sector", None), check_vma=False)
```

```python
import functools

import jax
import jax.numpy as jnp
from jax import lax
from jax.experimental import pallas as pl
from jax.experimental.pallas import tpu as pltpu
from jax.sharding import PartitionSpec as P

MESH = pl.DeviceIdType.MESH
PIECE = 32
LAG = 4
SHARED = 0.6


def kernel(n_s, n_t, pieces, part, cuts, blocks_ref, left_ref, right_ref, coup_ref, width_ref, out_ref,
           lbuf, rbuf, st1, st2, tbuf, sbuf, recv, send, obuf,
           lsem, osem, h1s, h1r, shs, shr, ups, upr, dns, dnr, rss, rsr, ags, agr, h2s, h2r):
    s = lax.axis_index("sector")
    z = lax.axis_index("term")
    side = blocks_ref.shape[0]
    half = side // 2
    pr = half // pieces
    has_lo, has_hi = s > 0, s < n_s - 1
    has_dn, has_up = z > 0, z < n_t - 1

    def to_sector(d):
        return (s + d, z)

    own1 = st1.at[pl.ds(side, side), :]
    cp_own = pltpu.make_async_copy(blocks_ref, own1, lsem.at[0])
    cp_l = pltpu.make_async_copy(left_ref.at[0, 0], lbuf, lsem.at[1])
    cp_r = pltpu.make_async_copy(right_ref.at[0, 0], rbuf, lsem.at[2])
    cp_own.start()
    cp_l.start()
    cp_r.start()

    barrier = pltpu.get_barrier_semaphore()
    for cond, dev in ((has_lo, (s - 1, z)), (has_hi, (s + 1, z)), (has_dn, (s, z - 1)), (has_up, (s, z + 1))):
        @pl.when(cond)
        def _():
            pl.semaphore_signal(barrier, inc=1, device_id=dev, device_id_type=MESH)
    count = (has_lo.astype(jnp.int32) + has_hi.astype(jnp.int32)
             + has_dn.astype(jnp.int32) + has_up.astype(jnp.int32))
    pl.semaphore_wait(barrier, count)

    odd = lax.rem(s, 2)
    mate = s + 1 - 2 * odd
    far_s = s - 1 + 2 * odd
    has_far = (far_s >= 0) & (far_s < n_s)
    g_mate = 2 - 2 * odd
    g_far = 2 * odd
    direct = side - n_t * part
    cut = part // cuts

    def rows1(group, offset, size):
        return pl.ds(pl.multiple_of(group * side + offset, 16), size)

    def mate_copy():
        return pltpu.make_async_remote_copy(
            src_ref=blocks_ref, dst_ref=st1.at[rows1(2 - g_mate, 0, side), :],
            send_sem=h1s.at[0], recv_sem=h1r.at[0], device_id=(mate, z), device_id_type=MESH)

    def direct_copy():
        return pltpu.make_async_remote_copy(
            src_ref=blocks_ref.at[pl.ds(0, direct), :], dst_ref=st1.at[rows1(2 - g_far, 0, direct), :],
            send_sem=h1s.at[1], recv_sem=h1r.at[1], device_id=(far_s, z), device_id_type=MESH)

    def part_copy(q):
        offset = direct + z * part + q * cut
        return pltpu.make_async_remote_copy(
            src_ref=blocks_ref.at[pl.ds(pl.multiple_of(offset, 16), cut), :],
            dst_ref=st1.at[rows1(2 - g_far, offset, cut), :],
            send_sem=shs.at[q], recv_sem=shr.at[q], device_id=(far_s, z), device_id_type=MESH)

    def pass_copy(owner, q, d):
        ref = st1.at[rows1(g_far, direct + owner * part + q * cut, cut), :]
        sends, recvs = (ups, upr) if d > 0 else (dns, dnr)
        return pltpu.make_async_remote_copy(
            src_ref=ref, dst_ref=ref, send_sem=sends.at[owner, q], recv_sem=recvs.at[owner, q],
            device_id=(s, z + d), device_id_type=MESH)

    @pl.when(has_far)
    def _():
        for q in range(cuts):
            part_copy(q).start()
        direct_copy().start()
    mate_copy().start()

    zeros = jnp.zeros((side, side), st1.dtype)

    @pl.when(jnp.logical_not(has_lo))
    def _():
        st1[pl.ds(0, side), :] = zeros
        st2[pl.ds(0, side), :] = zeros

    @pl.when(jnp.logical_not(has_hi))
    def _():
        st1[pl.ds(2 * side, side), :] = zeros
        st2[pl.ds(2 * side, side), :] = zeros

    width = width_ref[0]
    cp_l.wait()
    for k in range(3):
        c = coup_ref[0, k].astype(jnp.float32)
        cols = pl.ds(k * side, side)
        lbuf[:, cols] = (lbuf[:, cols].astype(jnp.float32) * c).astype(lbuf.dtype)
    cp_own.wait()
    cp_r.wait()

    x = jnp.where(z * 2 < n_t, 1, 0)
    flows = (x, 1 - x)

    def far(f):
        return jnp.where(f == 1, z, n_t - 1 - z)

    def has_prev(f):
        return far(f) > 0

    def has_next(f):
        return jnp.where(f == 1, n_t - 1 - z, z) > 0

    def rows_of(f, i):
        return pl.ds(pl.multiple_of(f * half + i * pr, pr), pr)

    def cols_of(g):
        return pl.ds(pl.multiple_of(g * side, 128), side)

    def contract(st, f, a):
        base = pl.ds(pl.multiple_of(f * half, half), half)
        if a == 0:
            t = tbuf[base, :] + jnp.dot(
                lbuf[base, cols_of(g_far)], st[rows1(g_far, 0, side), :], preferred_element_type=jnp.float32)
        else:
            t = jnp.dot(lbuf[base, :], st[...], preferred_element_type=jnp.float32)
        sbuf[base, :] = jnp.dot(t.astype(jnp.bfloat16), rbuf[...], preferred_element_type=jnp.float32)

    def rs_copy(a, f, i):
        r = rows_of(f, i)
        return pltpu.make_async_remote_copy(
            src_ref=send.at[a, r, :], dst_ref=recv.at[a, r, :],
            send_sem=rss.at[a, f, i], recv_sem=rsr.at[a, f, i],
            device_id=(s, z + 2 * f - 1), device_id_type=MESH)

    def result(a, f, i):
        if a == 0:
            return st2.at[pl.ds(pl.multiple_of(side + f * half + i * pr, pr), pr), :]
        return obuf.at[rows_of(f, i), :]

    def ag_copy(a, f, i):
        return pltpu.make_async_remote_copy(
            src_ref=result(a, f, i), dst_ref=result(a, f, i),
            send_sem=ags.at[a, f, i], recv_sem=agr.at[a, f, i],
            device_id=(s, z - 2 * f + 1), device_id_type=MESH)

    def halo2(d, f, i):
        group = 2 if d < 0 else 0
        slot = 0 if d < 0 else 1
        dst = pl.ds(pl.multiple_of(group * side + f * half + i * pr, pr), pr)
        return pltpu.make_async_remote_copy(
            src_ref=result(0, f, i), dst_ref=st2.at[dst, :],
            send_sem=h2s.at[slot, f, i], recv_sem=h2r.at[slot, f, i],
            device_id=to_sector(d), device_id_type=MESH)

    def out_copy(f, i):
        return pltpu.make_async_copy(obuf.at[rows_of(f, i), :], out_ref.at[rows_of(f, i), :], osem.at[f, i])

    def publish(a, f, i):
        if a == 0:
            @pl.when(has_lo)
            def _():
                halo2(-1, f, i).start()

            @pl.when(has_hi)
            def _():
                halo2(1, f, i).start()
        else:
            out_copy(f, i).start()

    def reduce_step(a, f, i):
        r = rows_of(f, i)

        @pl.when(has_prev(f))
        def _():
            rs_copy(a, f, i).wait_recv()
            sbuf[r, :] = sbuf[r, :] + recv[a, r, :].astype(jnp.float32)

        @pl.when(has_next(f))
        def _():
            send[a, r, :] = sbuf[r, :].astype(send.dtype)
            rs_copy(a, f, i).start()

        @pl.when(jnp.logical_not(has_next(f)))
        def _():
            value = sbuf[r, :]
            row = f * half + i * pr + lax.broadcasted_iota(jnp.int32, value.shape, 0)
            col = lax.broadcasted_iota(jnp.int32, value.shape, 1)
            value = jnp.where((row < width) & (col < width), value, jnp.zeros_like(value))
            if a == 1:
                start = st1[pl.ds(pl.multiple_of(side + f * half + i * pr, pr), pr), :]
                value = 2.0 * value - start.astype(jnp.float32)
            result(a, f, i)[...] = value.astype(st2.dtype)

            @pl.when(has_prev(f))
            def _():
                ag_copy(a, f, i).start()
            publish(a, f, i)

    def gather_step(a, f, i):
        @pl.when(has_next(f))
        def _():
            ag_copy(a, f, i).wait_recv()

            @pl.when(has_prev(f))
            def _():
                ag_copy(a, f, i).start()
            publish(a, f, i)

    def loop(body):
        def step(i, c):
            body(i)
            return c
        lax.fori_loop(0, pieces, step, 0)

    def apply(a, st):
        fx, fy = flows
        contract(st, fx, a)

        @pl.when(jnp.logical_not(has_prev(fx)))
        def _():
            loop(lambda i: reduce_step(a, fx, i))

        contract(st, fy, a)

        def slot(t, c):
            for f in (fy, fx):
                i = t - (2 * (n_t - 1) - far(f)) * LAG

                @pl.when((i >= 0) & (i < pieces))
                def _():
                    gather_step(a, f, i)
            for f in (fy, fx):
                i = t - far(f) * LAG
                ready = (i >= 0) & (i < pieces)

                @pl.when(ready & has_prev(f) if f is fx else ready)
                def _():
                    reduce_step(a, f, i)
            return c
        lax.fori_loop(0, 2 * (n_t - 1) * LAG + pieces, slot, 0)

    @pl.when(has_far)
    def _():
        for q in range(cuts):
            part_copy(q).wait_recv()

            @pl.when(has_up)
            def _():
                pass_copy(z, q, 1).start()

            @pl.when(has_dn)
            def _():
                pass_copy(z, q, -1).start()

    mate_copy().wait_recv()
    for f in (0, 1):
        base = pl.ds(f * half, half)
        tbuf[base, :] = (
            jnp.dot(lbuf[base, pl.ds(side, side)], st1[pl.ds(side, side), :], preferred_element_type=jnp.float32)
            + jnp.dot(lbuf[base, cols_of(g_mate)], st1[rows1(g_mate, 0, side), :], preferred_element_type=jnp.float32))

    @pl.when(has_far)
    def _():
        def farther(k, c):
            for q in range(cuts):
                @pl.when(z - k >= 0)
                def _():
                    pass_copy(z - k, q, 1).wait_recv()

                    @pl.when(has_up)
                    def _():
                        pass_copy(z - k, q, 1).start()

                @pl.when(z + k < n_t)
                def _():
                    pass_copy(z + k, q, -1).wait_recv()

                    @pl.when(has_dn)
                    def _():
                        pass_copy(z + k, q, -1).start()
            return c
        lax.fori_loop(1, n_t, farther, 0)
        direct_copy().wait_recv()
    apply(0, st1)

    def arrived(i):
        for f in flows:
            @pl.when(has_lo)
            def _():
                halo2(1, f, i).wait_recv()

            @pl.when(has_hi)
            def _():
                halo2(-1, f, i).wait_recv()
    loop(arrived)
    apply(1, st2)

    def drain(i):
        for f in (0, 1):
            for a in (0, 1):
                @pl.when(has_next(f))
                def _():
                    rs_copy(a, f, i).wait_send()

                @pl.when(has_prev(f))
                def _():
                    ag_copy(a, f, i).wait_send()

            @pl.when(has_lo)
            def _():
                halo2(-1, f, i).wait_send()

            @pl.when(has_hi)
            def _():
                halo2(1, f, i).wait_send()
            out_copy(f, i).wait()
    loop(drain)

    mate_copy().wait_send()

    @pl.when(has_far)
    def _():
        direct_copy().wait_send()
        for q in range(cuts):
            part_copy(q).wait_send()

        def passed(owner, c):
            for q in range(cuts):
                @pl.when(has_up & (owner <= z))
                def _():
                    pass_copy(owner, q, 1).wait_send()

                @pl.when(has_dn & (owner >= z))
                def _():
                    pass_copy(owner, q, -1).wait_send()
            return c
        lax.fori_loop(0, n_t, passed, 0)


def shards(n_s, n_t, blocks, left_env, right_env, coupling, widths):
    side = blocks.shape[1]
    pieces = side // 2 // PIECE
    part = int(SHARED * side) // (16 * n_t) * 16
    cuts = max(q for q in (1, 2, 3) if part % (16 * q) == 0)
    dma = pltpu.SemaphoreType.DMA
    any_space = pl.BlockSpec(memory_space=pl.ANY)
    smem = pl.BlockSpec(memory_space=pltpu.SMEM)
    return pl.pallas_call(
        functools.partial(kernel, n_s, n_t, pieces, part, cuts),
        out_shape=jax.ShapeDtypeStruct(blocks.shape, blocks.dtype),
        in_specs=[any_space, any_space, any_space, smem, smem],
        out_specs=any_space,
        scratch_shapes=[
            pltpu.VMEM((side, 3 * side), jnp.bfloat16),
            pltpu.VMEM((side, side), jnp.bfloat16),
            pltpu.VMEM((3 * side, side), jnp.bfloat16),
            pltpu.VMEM((3 * side, side), jnp.bfloat16),
            pltpu.VMEM((side, side), jnp.float32),
            pltpu.VMEM((side, side), jnp.float32),
            pltpu.VMEM((2, side, side), jnp.bfloat16),
            pltpu.VMEM((2, side, side), jnp.bfloat16),
            pltpu.VMEM((side, side), jnp.bfloat16),
            dma((3,)), dma((2, pieces)), dma((2,)), dma((2,)),
            dma((cuts,)), dma((cuts,)),
            dma((n_t, cuts)), dma((n_t, cuts)), dma((n_t, cuts)), dma((n_t, cuts)),
            dma((2, 2, pieces)), dma((2, 2, pieces)),
            dma((2, 2, pieces)), dma((2, 2, pieces)),
            dma((2, 2, pieces)), dma((2, 2, pieces)),
        ],
        compiler_params=pltpu.CompilerParams(collective_id=0, has_side_effects=True),
    )(blocks, left_env, right_env, coupling, widths)


def solution(mesh):
    placed = (
        P("sector", None),
        P("sector", "term", None, None),
        P("sector", "term", None, None),
        P("sector", None),
        P("sector"),
    )
    body = functools.partial(shards, mesh.shape["sector"], mesh.shape["term"])
    return jax.shard_map(body, mesh=mesh, in_specs=placed, out_specs=P("sector", None), check_vma=False)
```

```python
import functools

import jax
import jax.numpy as jnp
from jax import lax
from jax.experimental import pallas as pl
from jax.experimental.pallas import tpu as pltpu
from jax.sharding import PartitionSpec as P

MESH = pl.DeviceIdType.MESH
PIECE = 32
LAG = 4
BLOCKS = 2
SHARED = 0.6


def kernel(n_s, n_t, pieces, part, cuts, blocks_ref, left_ref, right_ref, coup_ref, width_ref, out_ref,
           lbuf, rbuf, st1, st2, tbuf, sbuf, recv, send, obuf,
           lsem, osem, h1s, h1r, shs, shr, ups, upr, dns, dnr, rss, rsr, ags, agr, h2s, h2r):
    s = lax.axis_index("sector")
    z = lax.axis_index("term")
    side = blocks_ref.shape[0]
    half = side // 2
    pr = half // pieces
    has_lo, has_hi = s > 0, s < n_s - 1
    has_dn, has_up = z > 0, z < n_t - 1

    def to_sector(d):
        return (s + d, z)

    own1 = st1.at[pl.ds(side, side), :]
    cp_own = pltpu.make_async_copy(blocks_ref, own1, lsem.at[0])
    cp_l = pltpu.make_async_copy(left_ref.at[0, 0], lbuf, lsem.at[1])
    cp_r = pltpu.make_async_copy(right_ref.at[0, 0], rbuf, lsem.at[2])
    cp_own.start()
    cp_l.start()
    cp_r.start()

    barrier = pltpu.get_barrier_semaphore()
    for cond, dev in ((has_lo, (s - 1, z)), (has_hi, (s + 1, z)), (has_dn, (s, z - 1)), (has_up, (s, z + 1))):
        @pl.when(cond)
        def _():
            pl.semaphore_signal(barrier, inc=1, device_id=dev, device_id_type=MESH)
    count = (has_lo.astype(jnp.int32) + has_hi.astype(jnp.int32)
             + has_dn.astype(jnp.int32) + has_up.astype(jnp.int32))
    pl.semaphore_wait(barrier, count)

    odd = lax.rem(s, 2)
    mate = s + 1 - 2 * odd
    far_s = s - 1 + 2 * odd
    has_far = (far_s >= 0) & (far_s < n_s)
    g_mate = 2 - 2 * odd
    g_far = 2 * odd
    direct = side - n_t * part
    cut = part // cuts

    def rows1(group, offset, size):
        return pl.ds(pl.multiple_of(group * side + offset, 16), size)

    def mate_copy():
        return pltpu.make_async_remote_copy(
            src_ref=blocks_ref, dst_ref=st1.at[rows1(2 - g_mate, 0, side), :],
            send_sem=h1s.at[0], recv_sem=h1r.at[0], device_id=(mate, z), device_id_type=MESH)

    def direct_copy():
        return pltpu.make_async_remote_copy(
            src_ref=blocks_ref.at[pl.ds(0, direct), :], dst_ref=st1.at[rows1(2 - g_far, 0, direct), :],
            send_sem=h1s.at[1], recv_sem=h1r.at[1], device_id=(far_s, z), device_id_type=MESH)

    def part_copy(q):
        offset = direct + z * part + q * cut
        return pltpu.make_async_remote_copy(
            src_ref=blocks_ref.at[pl.ds(pl.multiple_of(offset, 16), cut), :],
            dst_ref=st1.at[rows1(2 - g_far, offset, cut), :],
            send_sem=shs.at[q], recv_sem=shr.at[q], device_id=(far_s, z), device_id_type=MESH)

    def pass_copy(owner, q, d):
        ref = st1.at[rows1(g_far, direct + owner * part + q * cut, cut), :]
        sends, recvs = (ups, upr) if d > 0 else (dns, dnr)
        return pltpu.make_async_remote_copy(
            src_ref=ref, dst_ref=ref, send_sem=sends.at[owner, q], recv_sem=recvs.at[owner, q],
            device_id=(s, z + d), device_id_type=MESH)

    @pl.when(has_far)
    def _():
        for q in range(cuts):
            part_copy(q).start()
        direct_copy().start()
    mate_copy().start()

    zeros = jnp.zeros((side, side), st1.dtype)

    @pl.when(jnp.logical_not(has_lo))
    def _():
        st1[pl.ds(0, side), :] = zeros
        st2[pl.ds(0, side), :] = zeros

    @pl.when(jnp.logical_not(has_hi))
    def _():
        st1[pl.ds(2 * side, side), :] = zeros
        st2[pl.ds(2 * side, side), :] = zeros

    width = width_ref[0]

    x = jnp.where(z * 2 < n_t, 1, 0)
    flows = (x, 1 - x)

    def far(f):
        return jnp.where(f == 1, z, n_t - 1 - z)

    def has_prev(f):
        return far(f) > 0

    def has_next(f):
        return jnp.where(f == 1, n_t - 1 - z, z) > 0

    def rows_of(f, i):
        return pl.ds(pl.multiple_of(f * half + i * pr, pr), pr)

    def cols_of(g):
        return pl.ds(pl.multiple_of(g * side, 128), side)

    block = half // BLOCKS

    def contract(st, f, j, a):
        base = pl.ds(pl.multiple_of(f * half + j * block, block), block)
        if a == 0:
            t = tbuf[base, :] + jnp.dot(
                lbuf[base, cols_of(g_far)], st[rows1(g_far, 0, side), :], preferred_element_type=jnp.float32)
        else:
            t = jnp.dot(lbuf[base, :], st[...], preferred_element_type=jnp.float32)
        sbuf[base, :] = jnp.dot(t.astype(jnp.bfloat16), rbuf[...], preferred_element_type=jnp.float32)

    def rs_copy(a, f, i):
        r = rows_of(f, i)
        return pltpu.make_async_remote_copy(
            src_ref=send.at[a, r, :], dst_ref=recv.at[a, r, :],
            send_sem=rss.at[a, f, i], recv_sem=rsr.at[a, f, i],
            device_id=(s, z + 2 * f - 1), device_id_type=MESH)

    def result(a, f, i):
        if a == 0:
            return st2.at[pl.ds(pl.multiple_of(side + f * half + i * pr, pr), pr), :]
        return obuf.at[rows_of(f, i), :]

    def ag_copy(a, f, i):
        return pltpu.make_async_remote_copy(
            src_ref=result(a, f, i), dst_ref=result(a, f, i),
            send_sem=ags.at[a, f, i], recv_sem=agr.at[a, f, i],
            device_id=(s, z - 2 * f + 1), device_id_type=MESH)

    def halo2(d, f, i):
        group = 2 if d < 0 else 0
        slot = 0 if d < 0 else 1
        dst = pl.ds(pl.multiple_of(group * side + f * half + i * pr, pr), pr)
        return pltpu.make_async_remote_copy(
            src_ref=result(0, f, i), dst_ref=st2.at[dst, :],
            send_sem=h2s.at[slot, f, i], recv_sem=h2r.at[slot, f, i],
            device_id=to_sector(d), device_id_type=MESH)

    def out_copy(f, i):
        return pltpu.make_async_copy(obuf.at[rows_of(f, i), :], out_ref.at[rows_of(f, i), :], osem.at[f, i])

    def publish(a, f, i):
        if a == 0:
            @pl.when(has_lo)
            def _():
                halo2(-1, f, i).start()

            @pl.when(has_hi)
            def _():
                halo2(1, f, i).start()
        else:
            out_copy(f, i).start()

    def reduce_step(a, f, i):
        r = rows_of(f, i)

        @pl.when(has_prev(f))
        def _():
            rs_copy(a, f, i).wait_recv()
            sbuf[r, :] = sbuf[r, :] + recv[a, r, :].astype(jnp.float32)

        @pl.when(has_next(f))
        def _():
            send[a, r, :] = sbuf[r, :].astype(send.dtype)
            rs_copy(a, f, i).start()

        @pl.when(jnp.logical_not(has_next(f)))
        def _():
            value = sbuf[r, :]
            row = f * half + i * pr + lax.broadcasted_iota(jnp.int32, value.shape, 0)
            col = lax.broadcasted_iota(jnp.int32, value.shape, 1)
            value = jnp.where((row < width) & (col < width), value, jnp.zeros_like(value))
            if a == 1:
                start = st1[pl.ds(pl.multiple_of(side + f * half + i * pr, pr), pr), :]
                value = 2.0 * value - start.astype(jnp.float32)
            result(a, f, i)[...] = value.astype(st2.dtype)

            @pl.when(has_prev(f))
            def _():
                ag_copy(a, f, i).start()
            publish(a, f, i)

    def gather_step(a, f, i):
        @pl.when(has_next(f))
        def _():
            ag_copy(a, f, i).wait_recv()

            @pl.when(has_prev(f))
            def _():
                ag_copy(a, f, i).start()
            publish(a, f, i)

    def loop(body):
        def step(i, c):
            body(i)
            return c
        lax.fori_loop(0, pieces, step, 0)

    def apply(a, st):
        fx, fy = flows
        def first(j, c):
            contract(st, fx, j, a)

            @pl.when(jnp.logical_not(has_prev(fx)))
            def _():
                for i in range(pieces // BLOCKS):
                    reduce_step(a, fx, j * (pieces // BLOCKS) + i)
            return c
        lax.fori_loop(0, BLOCKS, first, 0)

        def second(j, c):
            contract(st, fy, j, a)
            return c
        lax.fori_loop(0, BLOCKS, second, 0)

        def slot(t, c):
            for f in (fy, fx):
                i = t - (2 * (n_t - 1) - far(f)) * LAG

                @pl.when((i >= 0) & (i < pieces))
                def _():
                    gather_step(a, f, i)
            for f in (fy, fx):
                i = t - far(f) * LAG
                ready = (i >= 0) & (i < pieces)

                @pl.when(ready & has_prev(f) if f is fx else ready)
                def _():
                    reduce_step(a, f, i)
            return c
        lax.fori_loop(0, 2 * (n_t - 1) * LAG + pieces, slot, 0)

    @pl.when(has_far)
    def _():
        for q in range(cuts):
            part_copy(q).wait_recv()

            @pl.when(has_up)
            def _():
                pass_copy(z, q, 1).start()

            @pl.when(has_dn)
            def _():
                pass_copy(z, q, -1).start()

    def farther(k, c):
        for q in range(cuts):
            @pl.when(has_far & (z - k >= 0))
            def _():
                pass_copy(z - k, q, 1).wait_recv()

                @pl.when(has_up)
                def _():
                    pass_copy(z - k, q, 1).start()

            @pl.when(has_far & (z + k < n_t))
            def _():
                pass_copy(z + k, q, -1).wait_recv()

                @pl.when(has_dn)
                def _():
                    pass_copy(z + k, q, -1).start()
        return c

    def near(f):
        base = pl.ds(f * half, half)
        tbuf[base, :] = (
            jnp.dot(lbuf[base, pl.ds(side, side)], st1[pl.ds(side, side), :], preferred_element_type=jnp.float32)
            + jnp.dot(lbuf[base, cols_of(g_mate)], st1[rows1(g_mate, 0, side), :], preferred_element_type=jnp.float32))

    cp_l.wait()
    for k in range(3):
        c = coup_ref[0, k].astype(jnp.float32)
        cols = pl.ds(k * side, side)
        lbuf[:, cols] = (lbuf[:, cols].astype(jnp.float32) * c).astype(lbuf.dtype)
    cp_own.wait()
    cp_r.wait()
    mate_copy().wait_recv()
    farther(1, 0)
    near(0)
    lax.fori_loop(2, n_t, farther, 0)
    near(1)

    @pl.when(has_far)
    def _():
        direct_copy().wait_recv()
    apply(0, st1)

    def arrived(i):
        for f in flows:
            @pl.when(has_lo)
            def _():
                halo2(1, f, i).wait_recv()

            @pl.when(has_hi)
            def _():
                halo2(-1, f, i).wait_recv()
    loop(arrived)
    apply(1, st2)

    def drain(i):
        for f in (0, 1):
            for a in (0, 1):
                @pl.when(has_next(f))
                def _():
                    rs_copy(a, f, i).wait_send()

                @pl.when(has_prev(f))
                def _():
                    ag_copy(a, f, i).wait_send()

            @pl.when(has_lo)
            def _():
                halo2(-1, f, i).wait_send()

            @pl.when(has_hi)
            def _():
                halo2(1, f, i).wait_send()
            out_copy(f, i).wait()
    loop(drain)

    mate_copy().wait_send()

    @pl.when(has_far)
    def _():
        direct_copy().wait_send()
        for q in range(cuts):
            part_copy(q).wait_send()

        def passed(owner, c):
            for q in range(cuts):
                @pl.when(has_up & (owner <= z))
                def _():
                    pass_copy(owner, q, 1).wait_send()

                @pl.when(has_dn & (owner >= z))
                def _():
                    pass_copy(owner, q, -1).wait_send()
            return c
        lax.fori_loop(0, n_t, passed, 0)


def shards(n_s, n_t, blocks, left_env, right_env, coupling, widths):
    side = blocks.shape[1]
    pieces = side // 2 // PIECE
    part = int(SHARED * side) // (16 * n_t) * 16
    cuts = max(q for q in (1, 2, 3) if part % (16 * q) == 0)
    dma = pltpu.SemaphoreType.DMA
    any_space = pl.BlockSpec(memory_space=pl.ANY)
    smem = pl.BlockSpec(memory_space=pltpu.SMEM)
    return pl.pallas_call(
        functools.partial(kernel, n_s, n_t, pieces, part, cuts),
        out_shape=jax.ShapeDtypeStruct(blocks.shape, blocks.dtype),
        in_specs=[any_space, any_space, any_space, smem, smem],
        out_specs=any_space,
        scratch_shapes=[
            pltpu.VMEM((side, 3 * side), jnp.bfloat16),
            pltpu.VMEM((side, side), jnp.bfloat16),
            pltpu.VMEM((3 * side, side), jnp.bfloat16),
            pltpu.VMEM((3 * side, side), jnp.bfloat16),
            pltpu.VMEM((side, side), jnp.float32),
            pltpu.VMEM((side, side), jnp.float32),
            pltpu.VMEM((2, side, side), jnp.bfloat16),
            pltpu.VMEM((2, side, side), jnp.bfloat16),
            pltpu.VMEM((side, side), jnp.bfloat16),
            dma((3,)), dma((2, pieces)), dma((2,)), dma((2,)),
            dma((cuts,)), dma((cuts,)),
            dma((n_t, cuts)), dma((n_t, cuts)), dma((n_t, cuts)), dma((n_t, cuts)),
            dma((2, 2, pieces)), dma((2, 2, pieces)),
            dma((2, 2, pieces)), dma((2, 2, pieces)),
            dma((2, 2, pieces)), dma((2, 2, pieces)),
        ],
        compiler_params=pltpu.CompilerParams(collective_id=0, has_side_effects=True),
    )(blocks, left_env, right_env, coupling, widths)


def solution(mesh):
    placed = (
        P("sector", None),
        P("sector", "term", None, None),
        P("sector", "term", None, None),
        P("sector", None),
        P("sector"),
    )
    body = functools.partial(shards, mesh.shape["sector"], mesh.shape["term"])
    return jax.shard_map(body, mesh=mesh, in_specs=placed, out_specs=P("sector", None), check_vma=False)
```
